512 devices in a mesh: rep: 32 (over y, x), tp: 16 (over z, core).
Axes of the slice: x: 4, y: 8, z: 8, core: 2. Of those that a mesh axis runs over, the one named last changes fastest.
Arguments:
- hidden: bfloat16 [147456, 4096], P('rep', 'tp'), may hold values from -0.09375 to 0.09375
- out_grad: bfloat16 [147456, 512], P(('rep', 'tp')), may hold values from -6 to 6
- momentum: float32 [32, 4096, 512], P('rep', 'tp'), may hold values from -6 to 6
- band_rows: int32 [64, 8], P('tp'), may hold values from 0 to 48, as said below
- band_start_columns: int32 [64, 8], P('tp'), may hold values from 0 to 48, as said below
Outputs:
- momentum_out: float32 [32, 4096, 512], P('rep', 'tp')
- update: bfloat16 [4096, 512], P('tp')
The draws below stay inside these ranges and needn't reach their ends.
Inputs may be any that keep to these rules, and one draw needn't show every extreme that they name: `band_rows`: multiples of 16, the same for every replica. `band_start_columns`: multiples of 16, the same for every replica.
All inputs are finite; a program needn't handle non-finite values.
Results may differ from the reference program's by a relative error of at most 0.001.
Values may be sent and summed in bfloat16 or wider, within the bound.
A program may use at most 64 MiB of HBM per device.

```python
import jax
import jax.numpy as jnp
from jax import lax

TOK = 4608
CCH = 8
ALL_TOK = 147456
FFW = 4096
COLS = 512
CROWS = 64
N_REP = 32


def draw_band_rows(key, part):
    values = jax.random.randint(jax.random.fold_in(key, 11), (CROWS, CCH), 0, 4) * 16
    return values.at[0, 0].set(48).at[0, 1].set(0).astype(jnp.int32)


def draw_band_start_columns(key, part):
    values = jax.random.randint(jax.random.fold_in(key, 23), (CROWS, CCH), 0, 4) * 16
    return values.at[0, 0].set(0).at[0, 1].set(48).astype(jnp.int32)


def steps_of(own_key, shape, pieces, least, top_value):
    def one(dim, parts):
        draws = jax.random.uniform(jax.random.fold_in(jax.random.fold_in(own_key, 6), dim), (parts,), jnp.float32, least / len(pieces), top_value / len(pieces))
        return jnp.repeat(jnp.exp(draws), shape[dim] // parts).reshape((-1,) + (1,) * (len(shape) - dim - 1))

    loudness = one(*pieces[0])
    for cut in pieces[1:]:
        loudness = loudness * one(*cut)
    return loudness


def normal_values(rng, shape, width, limit, split=(), held_as=jnp.bfloat16):
    values = jax.random.normal(rng, shape, jnp.float32) * width
    if len(split) > 0:
        values = steps_of(rng, shape, split, -0.22, 0.18) * values
    return jnp.clip(values, min=-limit, max=limit).astype(held_as)


def setup_inputs(seed: int = 0) -> dict:
    seeds = jax.random.split(jax.random.key(seed), 6)
    hidden = normal_values(seeds[0], (ALL_TOK, FFW), TOK ** -0.5, 0.09375, ((0, 32), (1, 16)))
    out_grad = normal_values(seeds[1], (ALL_TOK, COLS), 1.0, 6.0, ((0, 512),))
    momentum = normal_values(seeds[2], (N_REP, FFW, COLS), 1.0, 6.0, ((0, 32), (1, 16)), jnp.float32)
    band_rows = draw_band_rows(jax.random.fold_in(seeds[5], 71), 0)
    band_start_columns = draw_band_start_columns(jax.random.fold_in(seeds[5], 71), 0)
    return {"hidden": hidden, "out_grad": out_grad, "momentum": momentum, "band_rows": band_rows, "band_start_columns": band_start_columns}


decay_rate = 0.9
highest_precision = lax.Precision.HIGHEST

def basis_matrix():
    frequency = jnp.arange(64, dtype=jnp.float32)[:, None]
    sample_pos = jnp.arange(64, dtype=jnp.float32)[None, :]
    norm_scale = jnp.where(frequency == 0, jnp.sqrt(jnp.float32(1.0 / 64)), jnp.sqrt(jnp.float32(2.0 / 64)))
    return norm_scale * jnp.cos(jnp.pi * (sample_pos + 0.5) * frequency / 64)

def reference(hidden, out_grad, momentum, band_rows, band_start_columns):
    basis = basis_matrix()
    tok_rows = hidden.shape[0] // N_REP
    row_count = hidden.shape[1]
    col_count = out_grad.shape[1]
    group_rows = row_count // 64
    group_cols = col_count // 64
    rows_flat = band_rows.reshape(-1).astype(jnp.int32)
    flattened_columns = band_start_columns.reshape(-1).astype(jnp.int32)

    def to_blocks(matrix):
        return matrix.reshape(group_rows, 64, group_cols, 64).transpose(0, 2, 1, 3).reshape(group_rows * group_cols, 64, 64)

    def from_blocks(blocks):
        return blocks.reshape(group_rows, group_cols, 64, 64).transpose(0, 2, 1, 3).reshape(row_count, col_count)
    inner_row = jnp.arange(64, dtype=jnp.int32)[None, :, None]
    inner_col = jnp.arange(64, dtype=jnp.int32)[None, None, :]
    inside = (inner_row >= rows_flat[:, None, None]) & (inner_row < rows_flat[:, None, None] + 16)
    inside = inside & (inner_col >= flattened_columns[:, None, None]) & (inner_col < flattened_columns[:, None, None] + 16)
    keep_mask = jnp.where(inside, jnp.float32(0.0), jnp.float32(1.0))

    def one_replica(replica):
        hidden_part = lax.dynamic_slice_in_dim(hidden, replica * tok_rows, tok_rows, 0)
        grad_part = lax.dynamic_slice_in_dim(out_grad, replica * tok_rows, tok_rows, 0)
        gradient = jnp.dot(hidden_part.T, grad_part, preferred_element_type=jnp.float32)
        merged = decay_rate * momentum[replica] + gradient
        coefficients = jnp.einsum('ij,cjk,lk->cil', basis, to_blocks(merged), basis, precision=highest_precision)
        frequency_bands = jax.vmap(lambda block, row_at, col_at: lax.dynamic_slice(block, (row_at, col_at), (16, 16)))(coefficients, rows_flat, flattened_columns)
        restored = jnp.einsum('ji,cjk,kl->cil', basis, coefficients * keep_mask, basis, precision=highest_precision)
        return (from_blocks(restored), frequency_bands)
    momentum_out, all_bands = lax.map(one_replica, jnp.arange(N_REP, dtype=jnp.int32))
    summed = lax.optimization_barrier(jnp.sum(all_bands, axis=0))
    placed = jax.vmap(lambda frequency_bands, row_at, col_at: lax.dynamic_update_slice(jnp.zeros((64, 64), jnp.float32), frequency_bands, (row_at, col_at)))(summed, rows_flat, flattened_columns)
    update = from_blocks(jnp.einsum('ji,cjk,kl->cil', basis, placed, basis, precision=highest_precision))
    return (momentum_out, update.astype(jnp.bfloat16))
```

```python
import functools

import jax
import jax.numpy as jnp
import numpy as np
from jax import lax
from jax.experimental import pallas as pl
from jax.experimental.pallas import tpu as pltpu
from jax.sharding import PartitionSpec as P

MESH = pl.DeviceIdType.MESH
NX = 4
NQ = 4
QW = 128
f32 = jnp.float32
bf16 = jnp.bfloat16


def block_basis():
    k = np.arange(64)[:, None].astype(np.float64)
    n = np.arange(64)[None, :].astype(np.float64)
    scale = np.where(k == 0, np.sqrt(1.0 / 64), np.sqrt(2.0 / 64))
    b = scale * np.cos(np.pi * (n + 0.5) * k / 64)
    return np.kron(np.eye(4), b).astype(np.float32)


def split(v):
    hi = v.astype(bf16)
    return hi, (v - hi.astype(f32)).astype(bf16)


def mm(a, b):
    return lax.dot_general(a, b, (((1,), (0,)), ((), ())), preferred_element_type=f32)


def mmt(a, b):
    return lax.dot_general(a, b, (((1,), (1,)), ((), ())), preferred_element_type=f32)


def mm3(dot, a, b):
    (ah, al), (bh, bl) = a, b
    return dot(ah, bh) + (dot(ah, bl) + dot(al, bh))


def kernel(
    dims, td,
    og, hid, mom, rows, cols, dmat,
    mom_out, upd_out,
    hperm, ht, o, g, rst, rt, wt, band, xbuf, xsum, ybuf, movm, updv,
    ring_s, ring_r, part_s, part_r, x_s, x_r, y_s, y_r, loc, out_s, greet,
):
    ny, nx, nz = dims
    ng = nz // 2
    rep = lax.axis_index("rep")
    tp = lax.axis_index("tp")
    y, x = rep // nx, rep % nx
    z, core = tp // 2, tp % 2
    toward = 1 - 2 * core

    def along_z(k):
        return (rep, lax.rem(z + k + nz, nz) * 2 + core)

    def along_x(k):
        return (y * nx + lax.rem(x + k + nx, nx), tp)

    def along_y(k):
        return (lax.rem(y + k + ny, ny) * nx + x, tp)

    partner = (rep, z * 2 + 1 - core)

    def local(src, dst, n):
        return pltpu.make_async_copy(src, dst, loc.at[n])

    own_o = [local(og.at[:, pl.ds(q * QW, QW)], o.at[q, ng - 1, pl.ds(0, td)], q) for q in range(NQ)]
    own_g = [local(mom.at[0, :, pl.ds(q * QW, QW)], g.at[q], NQ + q) for q in range(NQ)]
    own_h = []
    for gi in range(ng):
        for k in range(4):
            if gi < ng - 1:
                chip = z - (gi + 1) if k < 2 else z + (gi + 1)
            else:
                chip = z if k < 2 else z + nz // 2
            c = core if k % 2 == 0 else 1 - core
            t = lax.rem(chip + nz, nz) * 2 + c
            own_h.append(
                local(hid.at[pl.ds(pl.multiple_of(t * td, 32), td)], hperm.at[gi, pl.ds(k * td, td)], 2 * NQ + gi * 4 + k)
            )

    near = [along_z(1), along_z(-1), partner]
    if nx > 1:
        near += [along_x(1), along_x(-1)]
    if ny > 1:
        near += [along_y(1), along_y(-1)]
    barrier = pltpu.get_barrier_semaphore()
    for d in near:
        pl.semaphore_signal(barrier, inc=1, device_id=d, device_id_type=MESH)
    for c in own_h[:4]:
        c.start()
    for c in own_o:
        c.start()
    for c in own_g:
        c.start()
    for c in own_h[4:]:
        c.start()
    pl.semaphore_wait(barrier, len(near))

    sends = []

    def remote(src, dst, ss, rs, dev):
        return pltpu.make_async_remote_copy(
            src_ref=src, dst_ref=dst, send_sem=ss, recv_sem=rs, device_id=dev, device_id_type=MESH
        )

    def start(c):
        c.start()
        sends.append(c)

    def slot(q, gi, k):
        return o.at[q, gi, pl.ds(k * td, td)]

    def ring(q, h, side, src):
        if h < ng - 1:
            return remote(src, slot(q, h, 2 * side), ring_s.at[q, h, side], ring_r.at[q, h, side],
                          along_z(1 if side == 0 else -1))
        return remote(src, slot(q, ng - 1, 2), ring_s.at[q, h, 0], ring_r.at[q, h, 0], along_z(toward))

    def hand(q, gi, k, src):
        return remote(src, slot(q, gi, k + 1), part_s.at[q, gi, k // 2], part_r.at[q, gi, k // 2], partner)

    for q in range(NQ):
        src = og.at[:, pl.ds(q * QW, QW)]
        if ng > 1:
            start(ring(q, 0, 0, src))
            start(ring(q, 0, 1, src))
        else:
            start(ring(q, 0, 0, src))
        start(hand(q, ng - 1, 0, src))

    rounds = []
    if nx > 1:
        rounds += [(along_x, i) for i in range(nx // 2 - 1)]
    if ny > 1:
        rounds += [(along_y, i) for i in range(ny // 2 - 1)]
    for n, (axis, _) in enumerate(rounds):
        for s, k in enumerate((1, -1)):
            pl.semaphore_signal(greet.at[n, s], inc=1, device_id=axis(k), device_id_type=MESH)
        for s in range(2):
            pl.semaphore_wait(greet.at[n, s], 1)

    def turn(gi):
        for k in range(4):
            own_h[gi * 4 + k].wait()
        for j in range(4 * td // 128):
            ht[gi, :, pl.ds(j * 128, 128)] = jnp.transpose(hperm[gi, pl.ds(j * 128, 128), :])

    def pick(start_at, base, width):
        v = dmat[pl.ds(base, 16), pl.ds(0, width)]
        for t in range(1, 4):
            v = lax.select(start_at == 16 * t, dmat[pl.ds(base + 16 * t, 16), pl.ds(0, width)], v)
        return v

    def bases(q):
        wt[q] = jnp.zeros((2, 128, 512), bf16)
        for b in range(2):
            for a in range(4):
                r = pick(rows[a, 2 * q + b], 64 * a, 256)
                rh, rl = split(r)
                rst[q, 0, pl.ds(64 * b + 16 * a, 16)] = rh
                rst[q, 1, pl.ds(64 * b + 16 * a, 16)] = rl
                wh, wl = split(pick(cols[a, 2 * q + b], 64 * b, 128))
                wt[q, 0, pl.ds(32 * a + 16 * b, 16), pl.ds(128 * a, 128)] = wh
                wt[q, 1, pl.ds(32 * a + 16 * b, 16), pl.ds(128 * a, 128)] = wl
        rt[q, 0] = jnp.transpose(rst[q, 0])
        rt[q, 1] = jnp.transpose(rst[q, 1])

    def product(q, gi):
        return mm(ht[gi], o[q, gi])

    lane = lax.broadcasted_iota(jnp.int32, (64, 128), 1)

    def analyse(q):
        yst = mm3(mm, (rst[q, 0], rst[q, 1]), split(g[q]))
        yc = jnp.where(lane < 64, yst[0:64], yst[64:128])
        wide = jnp.concatenate([yc[16 * a:16 * a + 16] for a in range(4)], axis=1)
        return mm3(mmt, split(wide), (wt[q, 0], wt[q, 1]))

    def lift(q, bands):
        wide = mm3(mm, split(bands), (wt[q, 0], wt[q, 1]))
        yc = jnp.concatenate([wide[:, 128 * a:128 * a + 128] for a in range(4)], axis=0)
        stack = jnp.concatenate([jnp.where(lane < 64, yc, 0.0), jnp.where(lane < 64, 0.0, yc)], axis=0)
        return mm3(mm, (rt[q, 0], rt[q, 1]), split(stack))

    def x_copy(q, i):
        return remote(band.at[q], xbuf.at[q, x], x_s.at[q, i - 1], x_r.at[q, i - 1], along_x(i))

    def y_copy(q, i):
        return remote(xsum.at[q], ybuf.at[q, y], y_s.at[q, i - 1], y_r.at[q, i - 1], along_y(i))

    def x_send(q):
        v = analyse(q)
        band[q] = v
        for i in sorted(range(1, nx), key=lambda i: -min(i, nx - i)):
            start(x_copy(q, i))
        xbuf[q, x] = v

    def y_send(q):
        for i in range(1, nx):
            x_copy(q, i).wait_recv()
        s = xbuf[q, 0]
        for i in range(1, nx):
            s = s + xbuf[q, i]
        xsum[q] = s
        for i in sorted(range(1, ny), key=lambda i: -min(i, ny - i)):
            start(y_copy(q, i))
        ybuf[q, y] = s

    def mom_copy(q):
        return pltpu.make_async_copy(movm.at[q], mom_out.at[0, :, pl.ds(q * QW, QW)], out_s.at[q])

    def upd_copy(q):
        return pltpu.make_async_copy(updv.at[q], upd_out.at[:, pl.ds(q * QW, QW)], out_s.at[NQ + q])

    def keep(q):
        movm[q] = g[q] - lift(q, band[q])
        mom_copy(q).start()

    def finish(q):
        for i in range(1, ny):
            y_copy(q, i).wait_recv()
        s = ybuf[q, 0]
        for i in range(1, ny):
            s = s + ybuf[q, i]
        updv[q] = lift(q, s).astype(bf16)
        upd_copy(q).start()

    def arrive(q, h):
        if h < ng - 1:
            for side in range(2):
                here = slot(q, h, 2 * side)
                ring(q, h, side, here).wait_recv()
                if h + 1 < ng - 1:
                    start(ring(q, h + 1, side, here))
                start(hand(q, h, 2 * side, here))
            if h + 1 == ng - 1:
                start(ring(q, h + 1, 0, o.at[q, h, pl.ds(pl.multiple_of(core * 2 * td, 32), td)]))
        else:
            here = slot(q, h, 2)
            ring(q, h, 0, here).wait_recv()
            start(hand(q, h, 2, here))

    def gather(q, h):
        for k in (0, 2):
            hand(q, h, k, slot(q, h, k)).wait_recv()
        if h == ng - 1:
            own_o[q].wait()
        g[q] += product(q, h)

    turn(0)
    for q in range(NQ):
        own_g[q].wait()
        g[q] = 0.9 * g[q]

    extra = [functools.partial(bases, q) for q in range(NQ)]
    extra = [functools.partial(turn, gi) for gi in range(1, ng)] + extra
    prior = None
    for h in range(ng):
        for q in range(NQ):
            arrive(q, h)
            last = h == ng - 1 and q == 0
            while extra and (last or len(extra) > 0):
                extra.pop(0)()
                if not last:
                    break
            if prior is not None:
                gather(*prior)
                if prior[1] == ng - 1:
                    x_send(prior[0])
                    if prior[0] >= 2:
                        y_send(prior[0] - 2)
            prior = (q, h)
    gather(*prior)
    x_send(NQ - 1)
    y_send(NQ - 3)
    y_send(NQ - 2)
    keep(0)
    y_send(NQ - 1)
    for q in range(1, NQ):
        keep(q)
    for q in range(NQ):
        finish(q)
    for c in sends:
        c.wait_send()
    for q in range(NQ):
        mom_copy(q).wait()
        upd_copy(q).wait()


def build(dims, td):
    ny, nx, nz = dims
    ng = nz // 2
    dma = pltpu.SemaphoreType.DMA
    n_greet = max(1, (nx // 2 - 1 if nx > 1 else 0) + (ny // 2 - 1 if ny > 1 else 0))
    anyspace = pl.BlockSpec(memory_space=pl.ANY)
    return pl.pallas_call(
        functools.partial(kernel, dims, td),
        name="demo_step",
        out_shape=(
            jax.ShapeDtypeStruct((1, 256, 512), f32),
            jax.ShapeDtypeStruct((256, 512), bf16),
        ),
        in_specs=[
            anyspace, anyspace, anyspace,
            pl.BlockSpec(memory_space=pltpu.SMEM),
            pl.BlockSpec(memory_space=pltpu.SMEM),
            pl.BlockSpec(memory_space=pltpu.VMEM),
        ],
        out_specs=(anyspace, anyspace),
        scratch_shapes=[
            pltpu.VMEM((ng, 4 * td, 256), bf16),
            pltpu.VMEM((ng, 256, 4 * td), bf16),
            pltpu.VMEM((NQ, ng, 4 * td, QW), bf16),
            pltpu.VMEM((NQ, 256, QW), f32),
            pltpu.VMEM((NQ, 2, 128, 256), bf16),
            pltpu.VMEM((NQ, 2, 256, 128), bf16),
            pltpu.VMEM((NQ, 2, 128, 512), bf16),
            pltpu.VMEM((NQ, 16, 128), f32),
            pltpu.VMEM((NQ, nx, 16, 128), f32),
            pltpu.VMEM((NQ, 16, 128), f32),
            pltpu.VMEM((NQ, ny, 16, 128), f32),
            pltpu.VMEM((NQ, 256, QW), f32),
            pltpu.VMEM((NQ, 256, QW), bf16),
            dma((NQ, ng, 2)), dma((NQ, ng, 2)),
            dma((NQ, ng, 2)), dma((NQ, ng, 2)),
            dma((NQ, max(nx - 1, 1))), dma((NQ, max(nx - 1, 1))),
            dma((NQ, max(ny - 1, 1))), dma((NQ, max(ny - 1, 1))),
            dma((2 * NQ + 4 * ng,)),
            dma((2 * NQ,)),
            pltpu.SemaphoreType.REGULAR((n_greet, 2)),
        ],
        compiler_params=pltpu.CompilerParams(collective_id=0, has_side_effects=True),
    )


def solution(mesh):
    n_rep, n_tp = mesh.shape["rep"], mesh.shape["tp"]
    dims = (n_rep // NX, NX, n_tp // 2)

    def local(hidden, out_grad, momentum, band_rows, band_start_columns):
        call = build(dims, out_grad.shape[0])
        return call(out_grad, hidden, momentum, band_rows, band_start_columns, jnp.asarray(block_basis()))

    return jax.shard_map(
        local,
        mesh=mesh,
        in_specs=(
            P("rep", "tp"),
            P(("rep", "tp"), None),
            P("rep", "tp", None),
            P("tp", None),
            P("tp", None),
        ),
        out_specs=(P("rep", "tp", None), P("tp", None)),
        check_vma=False,
    )
```

```python
import functools

import jax
import jax.numpy as jnp
import numpy as np
from jax import lax
from jax.experimental import pallas as pl
from jax.experimental.pallas import tpu as pltpu
from jax.sharding import PartitionSpec as P

MESH = pl.DeviceIdType.MESH
NX = 4
NQ = 4
QW = 128
f32 = jnp.float32
bf16 = jnp.bfloat16


def block_basis():
    k = np.arange(64)[:, None].astype(np.float64)
    n = np.arange(64)[None, :].astype(np.float64)
    scale = np.where(k == 0, np.sqrt(1.0 / 64), np.sqrt(2.0 / 64))
    b = scale * np.cos(np.pi * (n + 0.5) * k / 64)
    return np.kron(np.eye(4), b).astype(np.float32)


def split(v):
    hi = v.astype(bf16)
    return hi, (v - hi.astype(f32)).astype(bf16)


def mm(a, b):
    return lax.dot_general(a, b, (((1,), (0,)), ((), ())), preferred_element_type=f32)


def mmt(a, b):
    return lax.dot_general(a, b, (((1,), (1,)), ((), ())), preferred_element_type=f32)


def mm3(dot, a, b):
    (ah, al), (bh, bl) = a, b
    return dot(ah, bh) + (dot(ah, bl) + dot(al, bh))


def kernel(
    dims, td,
    og, hid, mom, rows_any, cols_any, dmat_any,
    mom_out, upd_out,
    hperm, ht, o, g, rst, rt, wt, rh, yp, band, xbuf, xsum, ybuf, movm, updv, dmat, rows, cols,
    send_s, ring_r, part_r, x_r, y_r, loc, greet,
):
    ny, nx, nz = dims
    ng = nz // 2
    rep = lax.axis_index("rep")
    tp = lax.axis_index("tp")
    y, x = rep // nx, rep % nx
    z, core = tp // 2, tp % 2

    def from_right(chip):
        return jnp.logical_or(core == 1, lax.rem(chip + nz, nz) < nz // 8)

    go_right = jnp.logical_not(from_right(z + 1))
    go_left = from_right(z - 1)

    def along_z(k):
        return (rep, lax.rem(z + k + nz, nz) * 2 + core)

    def along_x(k):
        return (y * nx + lax.rem(x + k + nx, nx), tp)

    def along_y(k):
        return (lax.rem(y + k + ny, ny) * nx + x, tp)

    partner = (rep, z * 2 + 1 - core)

    def local(src, dst, n):
        return pltpu.make_async_copy(src, dst, loc.at[n])

    consts = [local(dmat_any, dmat, 0), local(rows_any, rows, 1), local(cols_any, cols, 2)]
    own_o = [local(og.at[:, pl.ds(q * QW, QW)], o.at[q, ng - 1, pl.ds(0, td)], 3) for q in range(NQ)]
    own_g = [local(mom.at[0, :, pl.ds(q * QW, QW)], g.at[q], 4) for q in range(NQ)]
    own_h = []
    for gi in range(ng):
        for k in range(4):
            if gi < ng - 1:
                chip = z - (gi + 1) if k % 2 == 0 else z + (gi + 1)
            else:
                chip = z if k % 2 == 0 else z + nz // 2
            c = core if k < 2 else 1 - core
            t = lax.rem(chip + nz, nz) * 2 + c
            own_h.append(
                local(hid.at[pl.ds(pl.multiple_of(t * td, 32), td)], hperm.at[gi, pl.ds(k * td, td)], 7 + gi)
            )

    def drain(view, sem):
        pltpu.make_async_copy(view, view, sem).wait()

    near = [along_z(1), along_z(-1), partner]
    if nx > 1:
        near += [along_x(1), along_x(-1)]
    if ny > 1:
        near += [along_y(1), along_y(-1)]
    barrier = pltpu.get_barrier_semaphore()
    for d in near:
        pl.semaphore_signal(barrier, inc=1, device_id=d, device_id_type=MESH)
    pl.semaphore_wait(barrier, len(near))

    def remote(src, dst, ss, rs, dev):
        return pltpu.make_async_remote_copy(
            src_ref=src, dst_ref=dst, send_sem=ss, recv_sem=rs, device_id=dev, device_id_type=MESH
        )

    def slot(q, gi, k):
        return o.at[q, gi, pl.ds(k * td, td)]

    def ring(q, h, side, src):
        return remote(src, slot(q, h, side), send_s.at[0], ring_r.at[q, 2 * h + side], along_z(1 - 2 * side))

    def far(q, side, src):
        return remote(src, slot(q, ng - 1, 1), send_s.at[1 + side], ring_r.at[q, 2 * ng - 2], along_z(1 - 2 * side))

    def hand(q, gi, k, src):
        return remote(src, slot(q, gi, k + 2), send_s.at[3], part_r.at[q, gi], partner)

    def send_far(q, sources):
        for side, go in enumerate((go_right, go_left)):
            @pl.when(go)
            def _(side=side):
                far(q, side, sources[side]).start()

    for q in range(NQ):
        src = og.at[:, pl.ds(q * QW, QW)]
        if ng > 1:
            ring(q, 0, 0, src).start()
            ring(q, 0, 1, src).start()
        else:
            send_far(q, (src, src))
        hand(q, ng - 1, 0, src).start()

    for c in consts + own_h[:4] + own_g + own_o + own_h[4:]:
        c.start()

    rounds = []
    if nx > 1:
        rounds += [(along_x, i) for i in range(nx // 2 - 1)]
    if ny > 1:
        rounds += [(along_y, i) for i in range(ny // 2 - 1)]
    for n, (axis, _) in enumerate(rounds):
        for k in (1, -1):
            pl.semaphore_signal(greet.at[n], inc=1, device_id=axis(k), device_id_type=MESH)
        pl.semaphore_wait(greet.at[n], 2)

    def turn(gi):
        drain(hperm.at[gi], loc.at[7 + gi])
        for j in range(4 * td // 128):
            ht[gi, :, pl.ds(j * 128, 128)] = jnp.transpose(hperm[gi, pl.ds(j * 128, 128), :])

    def pick(start_at, base, width):
        v = dmat[pl.ds(base, 16), pl.ds(0, width)]
        for t in range(1, 4):
            v = lax.select(start_at == 16 * t, dmat[pl.ds(base + 16 * t, 16), pl.ds(0, width)], v)
        return v

    def bases(q):
        wt[q] = jnp.zeros((2, 128, 512), bf16)
        for b in range(2):
            for a in range(4):
                r = pick(rows[a, 2 * q + b], 64 * a, 256)
                hi, lo = split(r)
                rst[q, 0, pl.ds(64 * b + 16 * a, 16)] = hi
                rst[q, 1, pl.ds(64 * b + 16 * a, 16)] = lo
                wh, wl = split(pick(cols[a, 2 * q + b], 64 * b, 128))
                wt[q, 0, pl.ds(32 * a + 16 * b, 16), pl.ds(128 * a, 128)] = wh
                wt[q, 1, pl.ds(32 * a + 16 * b, 16), pl.ds(128 * a, 128)] = wl
        rt[q, 0] = jnp.transpose(rst[q, 0])
        rt[q, 1] = jnp.transpose(rst[q, 1])
        v = mm(rst[q, 0], ht[ng - 1]) + mm(rst[q, 1], ht[ng - 1])
        rh[q, 0], rh[q, 1] = split(v)

    def product(q, gi):
        return mm(ht[gi], o[q, gi])

    lane = lax.broadcasted_iota(jnp.int32, (64, 128), 1)

    def partial(q):
        yp[q] = mm3(mm, (rst[q, 0], rst[q, 1]), split(g[q]))

    def analyse(q):
        last = o[q, ng - 1]
        yst = yp[q] + (mm(rh[q, 0], last) + mm(rh[q, 1], last))
        yc = jnp.where(lane < 64, yst[0:64], yst[64:128])
        wide = jnp.concatenate([yc[16 * a:16 * a + 16] for a in range(4)], axis=1)
        return mm3(mmt, split(wide), (wt[q, 0], wt[q, 1]))

    def lift(q, bands):
        wide = mm3(mm, split(bands), (wt[q, 0], wt[q, 1]))
        yc = jnp.concatenate([wide[:, 128 * a:128 * a + 128] for a in range(4)], axis=0)
        stack = jnp.concatenate([jnp.where(lane < 64, yc, 0.0), jnp.where(lane < 64, 0.0, yc)], axis=0)
        return mm3(mm, (rt[q, 0], rt[q, 1]), split(stack))

    def x_copy(q, i):
        return remote(band.at[q], xbuf.at[q, x], send_s.at[4], x_r.at[q], along_x(i))

    def y_copy(q, i):
        return remote(xsum.at[q], ybuf.at[q, y], send_s.at[5], y_r.at[q], along_y(i))

    def x_send(q):
        v = analyse(q)
        band[q] = v
        for i in sorted(range(1, nx), key=lambda i: -min(i, nx - i)):
            x_copy(q, i).start()
        xbuf[q, x] = v

    def y_send(q):
        if nx > 1:
            drain(xbuf.at[q, pl.ds(0, nx - 1)], x_r.at[q])
        s = xbuf[q, 0]
        for i in range(1, nx):
            s = s + xbuf[q, i]
        xsum[q] = s
        for i in sorted(range(1, ny), key=lambda i: -min(i, ny - i)):
            y_copy(q, i).start()
        ybuf[q, y] = s

    def mom_copy(q):
        return pltpu.make_async_copy(movm.at[q], mom_out.at[q], loc.at[5])

    def upd_copy(q):
        return pltpu.make_async_copy(updv.at[q], upd_out.at[q], loc.at[6])

    def keep(q):
        movm[q] = g[q] + product(q, ng - 1) - lift(q, band[q])
        mom_copy(q).start()

    def finish(q):
        if ny > 1:
            drain(ybuf.at[q, pl.ds(0, ny - 1)], y_r.at[q])
        s = ybuf[q, 0]
        for i in range(1, ny):
            s = s + ybuf[q, i]
        updv[q] = lift(q, s).astype(bf16)
        upd_copy(q).start()

    def arrive(q, h):
        if h < ng - 1:
            for side in range(2):
                here = slot(q, h, side)
                ring(q, h, side, here).wait_recv()
                if h + 1 < ng - 1:
                    ring(q, h + 1, side, here).start()
                hand(q, h, side, here).start()
            if h + 1 == ng - 1:
                send_far(q, (slot(q, h, 0), slot(q, h, 1)))
        else:
            here = slot(q, h, 1)
            far(q, 0, here).wait_recv()
            hand(q, h, 1, here).start()

    def gather(q, h):
        drain(o.at[q, h, pl.ds(2 * td, 2 * td)], part_r.at[q, h])
        if h < ng - 1:
            g[q] += product(q, h)
            if h == ng - 2:
                partial(q)

    for c in consts:
        c.wait()
    turn(0)
    drain(g, loc.at[4])
    for q in range(NQ):
        g[q] = 0.9 * g[q]
        if ng == 1:
            bases(q)
            partial(q)
    drain(o.at[:, ng - 1, pl.ds(0, td)], loc.at[3])

    extra = [functools.partial(turn, gi) for gi in range(1, ng)]
    if ng > 1:
        extra += [functools.partial(bases, q) for q in range(NQ)]
    prior = None
    for h in range(ng):
        for q in range(NQ):
            arrive(q, h)
            if extra and (h or ng == 1):
                extra.pop(0)()
                if ng < 4:
                    while extra:
                        extra.pop(0)()
            if prior is not None:
                gather(*prior)
                if prior[1] == ng - 1:
                    x_send(prior[0])
                    if prior[0] >= 2:
                        y_send(prior[0] - 2)
            prior = (q, h)
    gather(*prior)
    x_send(NQ - 1)
    y_send(NQ - 3)
    y_send(NQ - 2)
    keep(0)
    y_send(NQ - 1)
    for q in range(1, NQ):
        keep(q)
    for q in range(NQ):
        finish(q)
    if ng > 1:
        drain(o.at[:, pl.ds(0, ng - 1), pl.ds(0, 2 * td)], send_s.at[0])
    for side, go in enumerate((go_right, go_left)):
        @pl.when(go)
        def _(side=side):
            drain(o.at[:, ng - 1, pl.ds(0, td)], send_s.at[1 + side])
    drain(o.at[:, :, pl.ds(0, 2 * td)], send_s.at[3])
    if nx > 1:
        drain(xbuf.at[:, pl.ds(0, nx - 1)], send_s.at[4])
    if ny > 1:
        drain(ybuf.at[:, pl.ds(0, ny - 1)], send_s.at[5])
    drain(movm, loc.at[5])
    drain(updv, loc.at[6])


def out_kernel(mom_in, upd_in, mom_out, upd_out, sems):
    def copies(q):
        return (
            pltpu.make_async_copy(mom_in.at[q], mom_out.at[0, :, pl.ds(q * QW, QW)], sems.at[0, q]),
            pltpu.make_async_copy(upd_in.at[q], upd_out.at[:, pl.ds(q * QW, QW)], sems.at[1, q]),
        )

    for q in range(NQ):
        for c in copies(q):
            c.start()
    for q in range(NQ):
        for c in copies(q):
            c.wait()


def build(dims, td):
    ny, nx, nz = dims
    ng = nz // 2
    dma = pltpu.SemaphoreType.DMA
    n_greet = max(1, (nx // 2 - 1 if nx > 1 else 0) + (ny // 2 - 1 if ny > 1 else 0))
    anyspace = pl.BlockSpec(memory_space=pl.ANY)
    hbm = pl.BlockSpec(memory_space=pltpu.HBM)
    step = pl.pallas_call(
        functools.partial(kernel, dims, td),
        name="demo_step",
        out_shape=(
            jax.ShapeDtypeStruct((NQ, 256, QW), f32),
            jax.ShapeDtypeStruct((NQ, 256, QW), bf16),
        ),
        in_specs=[hbm] * 6,
        out_specs=(anyspace, anyspace),
        scratch_shapes=[
            pltpu.VMEM((ng, 4 * td, 256), bf16),
            pltpu.VMEM((ng, 256, 4 * td), bf16),
            pltpu.VMEM((NQ, ng, 4 * td, QW), bf16),
            pltpu.VMEM((NQ, 256, QW), f32),
            pltpu.VMEM((NQ, 2, 128, 256), bf16),
            pltpu.VMEM((NQ, 2, 256, 128), bf16),
            pltpu.VMEM((NQ, 2, 128, 512), bf16),
            pltpu.VMEM((NQ, 2, 128, 4 * td), bf16),
            pltpu.VMEM((NQ, 128, 128), f32),
            pltpu.VMEM((NQ, 16, 128), f32),
            pltpu.VMEM((NQ, nx, 16, 128), f32),
            pltpu.VMEM((NQ, 16, 128), f32),
            pltpu.VMEM((NQ, ny, 16, 128), f32),
            pltpu.VMEM((NQ, 256, QW), f32),
            pltpu.VMEM((NQ, 256, QW), bf16),
            pltpu.VMEM((256, 256), f32),
            pltpu.SMEM((4, 8), jnp.int32),
            pltpu.SMEM((4, 8), jnp.int32),
            dma((6,)),
            dma((NQ, 2 * ng - 1)),
            dma((NQ, ng)),
            dma((NQ,)),
            dma((NQ,)),
            dma((7 + ng,)),
            pltpu.SemaphoreType.REGULAR((n_greet,)),
        ],
        compiler_params=pltpu.CompilerParams(
            collective_id=0, has_side_effects=True, vmem_limit_bytes=28 * 2**20
        ),
    )
    out = pl.pallas_call(
        out_kernel,
        name="results_out",
        out_shape=(
            jax.ShapeDtypeStruct((1, 256, 512), f32),
            jax.ShapeDtypeStruct((256, 512), bf16),
        ),
        in_specs=[anyspace, anyspace],
        out_specs=(anyspace, anyspace),
        scratch_shapes=[dma((2, NQ))],
        compiler_params=pltpu.CompilerParams(vmem_limit_bytes=2**20),
    )
    return lambda *args: out(*step(*[pltpu.with_memory_space_constraint(a, pltpu.HBM) for a in args]))


def solution(mesh):
    n_rep, n_tp = mesh.shape["rep"], mesh.shape["tp"]
    dims = (n_rep // NX, NX, n_tp // 2)

    def local(hidden, out_grad, momentum, band_rows, band_start_columns):
        call = build(dims, out_grad.shape[0])
        return call(out_grad, hidden, momentum, band_rows, band_start_columns, jnp.asarray(block_basis()))

    return jax.shard_map(
        local,
        mesh=mesh,
        in_specs=(
            P("rep", "tp"),
            P(("rep", "tp"), None),
            P("rep", "tp", None),
            P("tp", None),
            P("tp", None),
        ),
        out_specs=(P("rep", "tp", None), P("tp", None)),
        check_vma=False,
    )
```

```python
import functools

import jax
import jax.numpy as jnp
import numpy as np
from jax import lax
from jax.experimental import pallas as pl
from jax.experimental.pallas import tpu as pltpu
from jax.sharding import PartitionSpec as P

MESH = pl.DeviceIdType.MESH
NX = 4
NQ = 4
QW = 128
Y_FIRST = (0, 1)
SECOND = (2, 3, 0, 1)
LAST = (0, 1, 2, 3)
f32 = jnp.float32
bf16 = jnp.bfloat16


def block_basis():
    k = np.arange(64)[:, None].astype(np.float64)
    n = np.arange(64)[None, :].astype(np.float64)
    scale = np.where(k == 0, np.sqrt(1.0 / 64), np.sqrt(2.0 / 64))
    b = scale * np.cos(np.pi * (n + 0.5) * k / 64)
    return np.kron(np.eye(4), b).astype(np.float32)


def split(v):
    hi = v.astype(bf16)
    return hi, (v - hi.astype(f32)).astype(bf16)


def mm(a, b):
    return lax.dot_general(a, b, (((1,), (0,)), ((), ())), preferred_element_type=f32)


def mmt(a, b):
    return lax.dot_general(a, b, (((1,), (1,)), ((), ())), preferred_element_type=f32)


def mm3(dot, a, b):
    (ah, al), (bh, bl) = a, b
    return dot(ah, bh) + (dot(ah, bl) + dot(al, bh))


def kernel(
    dims, td,
    og, hid, mom, rows_any, cols_any, dmat_any,
    mom_out, upd_out,
    hperm, ht, o, g, rst, rt, wk, wr, rh, yp, band, xbuf, xsum, ybuf, dmat, rows, cols,
    send_s, ring_r, part_r, x_r, y_r, loc, greet,
):
    ny, nx, nz = dims
    ng = nz // 2
    rep = lax.axis_index("rep")
    tp = lax.axis_index("tp")
    y, x = rep // nx, rep % nx
    z, core = tp // 2, tp % 2

    def from_right(chip):
        return jnp.logical_or(core == 1, lax.rem(chip + nz, nz) < nz // 8)

    go_right = jnp.logical_not(from_right(z + 1))
    go_left = from_right(z - 1)

    def along_z(k):
        return (rep, lax.rem(z + k + nz, nz) * 2 + core)

    def along_x(k):
        return (y * nx + lax.rem(x + k + nx, nx), tp)

    def along_y(k):
        return (lax.rem(y + k + ny, ny) * nx + x, tp)

    partner = (rep, z * 2 + 1 - core)

    def local(src, dst, n):
        return pltpu.make_async_copy(src, dst, loc.at[n])

    consts = [local(dmat_any, dmat, 0), local(rows_any, rows, 1), local(cols_any, cols, 2)]
    pad = -2 * td % 128

    def place(gi, k):
        if gi < ng - 1:
            return k * td
        return (0, 2 * td + pad, td, 3 * td + pad)[k]

    own_o = [local(og.at[:, pl.ds(q * QW, QW)], o.at[q, ng - 1, pl.ds(0, td)], 3) for q in range(NQ)]
    own_g = [local(mom.at[0, :, pl.ds(q * QW, QW)], g.at[q], 4) for q in range(NQ)]
    own_h = []
    for gi in range(ng):
        for k in range(4):
            if gi < ng - 1:
                chip = z - (gi + 1) if k % 2 == 0 else z + (gi + 1)
            else:
                chip = z if k % 2 == 0 else z + nz // 2
            c = core if k < 2 else 1 - core
            t = lax.rem(chip + nz, nz) * 2 + c
            own_h.append(
                local(hid.at[pl.ds(pl.multiple_of(t * td, 32), td)], hperm.at[gi, pl.ds(place(gi, k), td)], 5 + gi)
            )

    def drain(view, sem):
        pltpu.make_async_copy(view, view, sem).wait()

    near = [along_z(1), along_z(-1), partner]
    if nx > 1:
        near += [along_x(1), along_x(-1)]
    if ny > 1:
        near += [along_y(1), along_y(-1)]
    barrier = pltpu.get_barrier_semaphore()
    for d in near:
        pl.semaphore_signal(barrier, inc=1, device_id=d, device_id_type=MESH)
    pl.semaphore_wait(barrier, len(near))

    def remote(src, dst, ss, rs, dev):
        return pltpu.make_async_remote_copy(
            src_ref=src, dst_ref=dst, send_sem=ss, recv_sem=rs, device_id=dev, device_id_type=MESH
        )

    def slot(q, gi, k):
        return o.at[q, gi, pl.ds(place(gi, k), td)]

    def ring(q, h, side, src):
        return remote(src, slot(q, h, side), send_s.at[0], ring_r.at[q, 2 * h + side], along_z(1 - 2 * side))

    def far(q, side, src):
        return remote(src, slot(q, ng - 1, 1), send_s.at[1 + side], ring_r.at[q, 2 * ng - 2], along_z(1 - 2 * side))

    def hand(q, gi, k, src):
        own = gi == ng - 1 and k == 0
        return remote(src, slot(q, gi, k + 2), send_s.at[3], loc.at[5 + ng + q] if own else part_r.at[q, gi], partner)

    def send_far(q, sources):
        for side, go in enumerate((go_right, go_left)):
            @pl.when(go)
            def _(side=side):
                far(q, side, sources[side]).start()

    for q in range(NQ):
        src = og.at[:, pl.ds(q * QW, QW)]
        if ng > 1:
            ring(q, 0, 0, src).start()
            ring(q, 0, 1, src).start()
        else:
            send_far(q, (src, src))
        hand(q, ng - 1, 0, src).start()

    for c in consts + own_h[:4] + own_g + own_o + own_h[4:]:
        c.start()

    rounds = []
    if nx > 1:
        rounds += [(along_x, i) for i in range(nx // 2 - 1)]
    if ny > 1:
        rounds += [(along_y, i) for i in range(ny // 2 - 1)]
    for n, (axis, _) in enumerate(rounds):
        for k in (1, -1):
            pl.semaphore_signal(greet.at[n], inc=1, device_id=axis(k), device_id_type=MESH)
        pl.semaphore_wait(greet.at[n], 2)

    def turn(gi):
        drain(hperm.at[gi, pl.ds(0, 4 * td)], loc.at[5 + gi])
        for j in range((4 * td if gi < ng - 1 else 4 * td + 2 * pad) // 128):
            ht[gi, :, pl.ds(j * 128, 128)] = jnp.transpose(hperm[gi, pl.ds(j * 128, 128), :])

    def pick(start_at, base, width):
        v = dmat[pl.ds(base, 16), pl.ds(0, width)]
        for t in range(1, 4):
            v = lax.select(start_at == 16 * t, dmat[pl.ds(base + 16 * t, 16), pl.ds(0, width)], v)
        return v

    def bases(q):
        for b in range(2):
            for a in range(4):
                hi, lo = split(pick(rows[a, 2 * q + b], 64 * a, 256))
                rst[q, 0, pl.ds(64 * b + 16 * a, 16)] = hi
                rst[q, 1, pl.ds(64 * b + 16 * a, 16)] = lo
                hi, lo = split(pick(cols[a, 2 * q + b], 64 * b, 128))
                for n, v in enumerate((hi, hi, lo)):
                    at = 32 * a + 16 * b
                    wk[q, pl.ds(at, 16), pl.ds(128 * n, 128)] = v
                    wr[q, pl.ds(128 * n + at, 16)] = v
        hi, lo = jnp.transpose(rst[q, 0]), jnp.transpose(rst[q, 1])
        for n, v in enumerate((hi, lo, hi)):
            rt[q, :, pl.ds(128 * n, 128)] = v
        far_h = ht[ng - 1, :, pl.ds(2 * td + pad, 2 * td)]
        hi, lo = split(mm(rst[q, 0], far_h) + mm(rst[q, 1], far_h))
        rh[q, pl.ds(0, 128)] = hi
        rh[q, pl.ds(128, 128)] = lo

    lane = lax.broadcasted_iota(jnp.int32, (64, 128), 1)
    lane16 = lax.broadcasted_iota(jnp.int32, (16, 128), 1)

    def of_row(a, v):
        return jnp.where(jnp.logical_and(lane16 >= 32 * a, lane16 < 32 * a + 32), v, 0.0)

    def near_part(q):
        g[q] += mm(ht[ng - 1, :, pl.ds(0, 2 * td)], o[q, ng - 1, pl.ds(0, 2 * td)])

    def far_part(q):
        far_h = ht[ng - 1, :, pl.ds(2 * td + pad, 2 * td)]
        return mm(far_h, o[q, ng - 1, pl.ds(2 * td + pad, 2 * td)])

    def partial(q):
        yp[q] = mm3(mm, (rst[q, 0], rst[q, 1]), split(g[q]))

    def analyse(q):
        v = mm(rh[q], o[q, ng - 1, pl.ds(2 * td + pad, 2 * td)])
        yst = yp[q] + (v[0:128] + v[128:256])
        hi, lo = split(jnp.where(lane < 64, yst[0:64], yst[64:128]))
        v = mmt(jnp.concatenate([hi, lo, hi], axis=1), wk[q])
        return sum(of_row(a, v[16 * a:16 * a + 16]) for a in range(1, 4)) + of_row(0, v[0:16])

    def lift(q, bands):
        hi, lo = split(jnp.concatenate([of_row(a, bands) for a in range(4)], axis=0))
        v = mm(jnp.concatenate([hi, lo, hi], axis=1), wr[q])
        v = jnp.concatenate([jnp.where(lane < 64, v, 0.0), jnp.where(lane < 64, 0.0, v)], axis=0)
        hi, lo = split(v)
        return mm(rt[q], jnp.concatenate([hi, hi, lo], axis=0))

    def axis(q, phase):
        return "y" if (q in Y_FIRST) == (phase == 0) else "x"

    def peer(name, i):
        return along_x(i) if name == "x" else along_y(i)

    size = {"x": nx, "y": ny}
    inbox = {"x": xbuf, "y": ybuf}
    place_of = {"x": x, "y": y}
    arrived = {"x": x_r, "y": y_r}
    sent = {"x": send_s.at[4], "y": send_s.at[5]}

    def spread(q, phase, src, value):
        name = axis(q, phase)
        n = size[name]
        for i in sorted(range(1, n), key=lambda i: -min(i, n - i)):
            remote(src.at[q], inbox[name].at[q, place_of[name]], sent[name], arrived[name].at[q], peer(name, i)).start()
        inbox[name][q, place_of[name]] = value

    def collect(q, phase):
        name = axis(q, phase)
        n, buf = size[name], inbox[name]
        if n > 1:
            drain(buf.at[q, pl.ds(0, n - 1)], arrived[name].at[q])
        s = buf[q, 0]
        for i in range(1, n):
            s = s + buf[q, i]
        return s

    def first_phase(q):
        v = analyse(q)
        band[q] = v
        spread(q, 0, band, v)

    def second_phase(q):
        s = collect(q, 0)
        xsum[q] = s
        spread(q, 1, xsum, s)

    def keep(q):
        mom_out[q] = g[q] + far_part(q) - lift(q, band[q])

    def finish(q):
        upd_out[q] = lift(q, collect(q, 1)).astype(bf16)

    def arrive(q, h):
        if h < ng - 1:
            for side in range(2):
                here = slot(q, h, side)
                ring(q, h, side, here).wait_recv()
                if h + 1 < ng - 1:
                    ring(q, h + 1, side, here).start()
                hand(q, h, side, here).start()
            if h + 1 == ng - 1:
                send_far(q, (slot(q, h, 0), slot(q, h, 1)))
        else:
            here = slot(q, h, 1)
            far(q, 0, here).wait_recv()
            hand(q, h, 1, here).start()

    def gather(q, h):
        if h < ng - 1:
            drain(o.at[q, h, pl.ds(2 * td, 2 * td)], part_r.at[q, h])
            g[q] += mm(ht[h, :, pl.ds(0, 4 * td)], o[q, h, pl.ds(0, 4 * td)])
            if h == ng - 2:
                partial(q)
        else:
            drain(slot(q, h, 3), part_r.at[q, h])

    for c in consts:
        c.wait()
    turn(ng - 1)
    drain(g, loc.at[4])
    drain(o.at[:, ng - 1, pl.ds(0, td)], loc.at[3])
    for q in range(NQ):
        drain(slot(q, ng - 1, 2), loc.at[5 + ng + q])
        g[q] = 0.9 * g[q]
        near_part(q)
        if ng == 1:
            bases(q)
            partial(q)

    extra = [functools.partial(turn, gi) for gi in range(1, ng - 1)]
    if ng > 1:
        turn(0)
        extra += [functools.partial(bases, q) for q in range(NQ)]
    prior = None
    for h in range(ng):
        for q in range(NQ):
            arrive(q, h)
            if extra and (h or ng == 1):
                extra.pop(0)()
                if ng < 4:
                    while extra:
                        extra.pop(0)()
            if prior is not None:
                gather(*prior)
                if prior[1] == ng - 1:
                    first_phase(prior[0])
            prior = (q, h)
    gather(*prior)
    first_phase(NQ - 1)
    keep(0)
    for q in SECOND:
        second_phase(q)
    for q in range(1, NQ):
        keep(q)
    for q in LAST:
        finish(q)
    if ng > 1:
        drain(o.at[:, pl.ds(0, ng - 1), pl.ds(0, 2 * td)], send_s.at[0])
    for side, go in enumerate((go_right, go_left)):
        @pl.when(go)
        def _(side=side):
            drain(o.at[:, ng - 1, pl.ds(0, td)], send_s.at[1 + side])
    drain(o.at[:, :, pl.ds(0, 2 * td)], send_s.at[3])
    if nx > 1:
        drain(xbuf.at[:, pl.ds(0, nx - 1)], send_s.at[4])
    if ny > 1:
        drain(ybuf.at[:, pl.ds(0, ny - 1)], send_s.at[5])


def out_kernel(mom_in, upd_in, mom_out, upd_out, sems):
    def copies(q):
        return (
            pltpu.make_async_copy(mom_in.at[q], mom_out.at[0, :, pl.ds(q * QW, QW)], sems.at[0, q]),
            pltpu.make_async_copy(upd_in.at[q], upd_out.at[:, pl.ds(q * QW, QW)], sems.at[1, q]),
        )

    for q in range(NQ):
        for c in copies(q):
            c.start()
    for q in range(NQ):
        for c in copies(q):
            c.wait()


def build(dims, td):
    ny, nx, nz = dims
    ng = nz // 2
    dma = pltpu.SemaphoreType.DMA
    n_greet = max(1, (nx // 2 - 1 if nx > 1 else 0) + (ny // 2 - 1 if ny > 1 else 0))
    rows_all = 4 * td + 2 * (-2 * td % 128)
    anyspace = pl.BlockSpec(memory_space=pl.ANY)
    hbm = pl.BlockSpec(memory_space=pltpu.HBM)
    vmem = pl.BlockSpec(memory_space=pltpu.VMEM)
    step = pl.pallas_call(
        functools.partial(kernel, dims, td),
        name="demo_step",
        out_shape=(
            jax.ShapeDtypeStruct((NQ, 256, QW), f32),
            jax.ShapeDtypeStruct((NQ, 256, QW), bf16),
        ),
        in_specs=[hbm] * 6,
        out_specs=(vmem, vmem),
        scratch_shapes=[
            pltpu.VMEM((ng, rows_all, 256), bf16),
            pltpu.VMEM((ng, 256, rows_all), bf16),
            pltpu.VMEM((NQ, ng, rows_all, QW), bf16),
            pltpu.VMEM((NQ, 256, QW), f32),
            pltpu.VMEM((NQ, 2, 128, 256), bf16),
            pltpu.VMEM((NQ, 256, 384), bf16),
            pltpu.VMEM((NQ, 128, 384), bf16),
            pltpu.VMEM((NQ, 384, 128), bf16),
            pltpu.VMEM((NQ, 256, 2 * td), bf16),
            pltpu.VMEM((NQ, 128, 128), f32),
            pltpu.VMEM((NQ, 16, 128), f32),
            pltpu.VMEM((NQ, nx, 16, 128), f32),
            pltpu.VMEM((NQ, 16, 128), f32),
            pltpu.VMEM((NQ, ny, 16, 128), f32),
            pltpu.VMEM((256, 256), f32),
            pltpu.SMEM((4, 8), jnp.int32),
            pltpu.SMEM((4, 8), jnp.int32),
            dma((6,)),
            dma((NQ, 2 * ng - 1)),
            dma((NQ, ng)),
            dma((NQ,)),
            dma((NQ,)),
            dma((5 + ng + NQ,)),
            pltpu.SemaphoreType.REGULAR((n_greet,)),
        ],
        compiler_params=pltpu.CompilerParams(
            collective_id=0, has_side_effects=True, vmem_limit_bytes=28 * 2**20
        ),
    )
    out = pl.pallas_call(
        out_kernel,
        name="results_out",
        out_shape=(
            jax.ShapeDtypeStruct((1, 256, 512), f32),
            jax.ShapeDtypeStruct((256, 512), bf16),
        ),
        in_specs=[anyspace, anyspace],
        out_specs=(anyspace, anyspace),
        scratch_shapes=[dma((2, NQ))],
        compiler_params=pltpu.CompilerParams(vmem_limit_bytes=2**20),
    )
    return lambda *args: out(*step(*[pltpu.with_memory_space_constraint(a, pltpu.HBM) for a in args]))


def solution(mesh):
    n_rep, n_tp = mesh.shape["rep"], mesh.shape["tp"]
    dims = (n_rep // NX, NX, n_tp // 2)

    def local(hidden, out_grad, momentum, band_rows, band_start_columns):
        call = build(dims, out_grad.shape[0])
        return call(out_grad, hidden, momentum, band_rows, band_start_columns, jnp.asarray(block_basis()))

    return jax.shard_map(
        local,
        mesh=mesh,
        in_specs=(
            P("rep", "tp"),
            P(("rep", "tp"), None),
            P("rep", "tp", None),
            P("tp", None),
            P("tp", None),
        ),
        out_specs=(P("rep", "tp", None), P("tp", None)),
        check_vma=False,
    )
```

```python
import functools

import jax
import jax.numpy as jnp
import numpy as np
from jax import lax
from jax.experimental import pallas as pl
from jax.experimental.pallas import tpu as pltpu
from jax.sharding import PartitionSpec as P

MESH = pl.DeviceIdType.MESH
NX = 4
NQ = 4
QW = 128
PARTS = 4
Y_FIRST = (0, 1)
SECOND = (2, 3, 0, 1)
LAST = (0, 1, 2, 3)
f32 = jnp.float32
bf16 = jnp.bfloat16


def block_basis():
    k = np.arange(64)[:, None].astype(np.float64)
    n = np.arange(64)[None, :].astype(np.float64)
    scale = np.where(k == 0, np.sqrt(1.0 / 64), np.sqrt(2.0 / 64))
    b = scale * np.cos(np.pi * (n + 0.5) * k / 64)
    return np.kron(np.eye(4), b).astype(np.float32)


def split(v):
    hi = v.astype(bf16)
    return hi, (v - hi.astype(f32)).astype(bf16)


def mm(a, b):
    return lax.dot_general(a, b, (((1,), (0,)), ((), ())), preferred_element_type=f32)


def mmt(a, b):
    return lax.dot_general(a, b, (((1,), (1,)), ((), ())), preferred_element_type=f32)


def mm3(dot, a, b):
    (ah, al), (bh, bl) = a, b
    return dot(ah, bh) + (dot(ah, bl) + dot(al, bh))


def kernel(
    dims, td,
    og, hid, mom, rows_any, cols_any, dmat_any,
    mom_out, upd_out,
    hperm, ht, o, g, rst, rt, wk, wr, rh, yp, band, xbuf, xsum, ybuf, dmat, rows, cols,
    send_s, ring_r, part_r, x_r, y_r, loc, greet,
):
    ny, nx, nz = dims
    ng = nz // 2
    rep = lax.axis_index("rep")
    tp = lax.axis_index("tp")
    y, x = rep // nx, rep % nx
    z, core = tp // 2, tp % 2

    def from_right(chip):
        return jnp.logical_or(core == 1, lax.rem(chip + nz, nz) < nz // 8)

    go_right = jnp.logical_not(from_right(z + 1))
    go_left = from_right(z - 1)

    def along_z(k):
        return (rep, lax.rem(z + k + nz, nz) * 2 + core)

    def along_x(k):
        return (y * nx + lax.rem(x + k + nx, nx), tp)

    def along_y(k):
        return (lax.rem(y + k + ny, ny) * nx + x, tp)

    partner = (rep, z * 2 + 1 - core)

    def local(src, dst, n):
        return pltpu.make_async_copy(src, dst, loc.at[n])

    consts = [local(dmat_any, dmat, 0), local(rows_any, rows, 1), local(cols_any, cols, 2)]
    pad = -2 * td % 128

    def place(gi, k):
        if gi < ng - 1:
            return k * td
        return (0, 2 * td + pad, td, 3 * td + pad)[k]

    own_o = [local(og.at[:, pl.ds(q * QW, QW)], o.at[q, ng - 1, pl.ds(0, td)], 3) for q in range(NQ)]
    own_g = [local(mom.at[0, :, pl.ds(q * QW, QW)], g.at[q], 4) for q in range(NQ)]
    own_h = []
    for gi in range(ng):
        for k in range(4):
            if gi < ng - 1:
                chip = z - (gi + 1) if k % 2 == 0 else z + (gi + 1)
            else:
                chip = z if k % 2 == 0 else z + nz // 2
            c = core if k < 2 else 1 - core
            t = lax.rem(chip + nz, nz) * 2 + c
            own_h.append(
                local(hid.at[pl.ds(pl.multiple_of(t * td, 32), td)], hperm.at[gi, pl.ds(place(gi, k), td)], 5 + gi)
            )

    def drain(view, sem):
        pltpu.make_async_copy(view, view, sem).wait()

    near = [along_z(1), along_z(-1), partner]
    if nx > 1:
        near += [along_x(1), along_x(-1)]
    if ny > 1:
        near += [along_y(1), along_y(-1)]
    barrier = pltpu.get_barrier_semaphore()
    for d in near:
        pl.semaphore_signal(barrier, inc=1, device_id=d, device_id_type=MESH)
    pl.semaphore_wait(barrier, len(near))

    def remote(src, dst, ss, rs, dev):
        return pltpu.make_async_remote_copy(
            src_ref=src, dst_ref=dst, send_sem=ss, recv_sem=rs, device_id=dev, device_id_type=MESH
        )

    def slot(q, gi, k):
        return o.at[q, gi, pl.ds(place(gi, k), td)]

    def ring(q, h, side, src):
        return remote(src, slot(q, h, side), send_s.at[0], ring_r.at[q, 2 * h + side], along_z(1 - 2 * side))

    def far(q, side, src):
        return remote(src, slot(q, ng - 1, 1), send_s.at[1 + side], ring_r.at[q, 2 * ng - 2], along_z(1 - 2 * side))

    def hand(q, gi, k, src):
        own = gi == ng - 1 and k == 0
        return remote(src, slot(q, gi, k + 2), send_s.at[3], loc.at[5 + ng] if own else part_r.at[q, gi], partner)

    def send_far(q, sources):
        for side, go in enumerate((go_right, go_left)):
            @pl.when(go)
            def _(side=side):
                far(q, side, sources[side]).start()

    for q in range(NQ):
        src = og.at[:, pl.ds(q * QW, QW)]
        if ng > 1:
            ring(q, 0, 0, src).start()
            ring(q, 0, 1, src).start()
        else:
            send_far(q, (src, src))
        hand(q, ng - 1, 0, src).start()

    for c in consts + own_h[:4] + own_g + own_o + own_h[4:]:
        c.start()

    rounds = []
    if nx > 1:
        rounds += [(along_x, i) for i in range(nx // 2 - 1)]
    if ny > 1:
        rounds += [(along_y, i) for i in range(ny // 2 - 1)]
    for n, (axis, _) in enumerate(rounds):
        for k in (1, -1):
            pl.semaphore_signal(greet.at[n], inc=1, device_id=axis(k), device_id_type=MESH)
        pl.semaphore_wait(greet.at[n], 2)

    def turn(gi):
        drain(hperm.at[gi, pl.ds(0, 4 * td)], loc.at[5 + gi])
        for j in range((4 * td if gi < ng - 1 else 4 * td + 2 * pad) // 128):
            ht[gi, :, pl.ds(j * 128, 128)] = jnp.transpose(hperm[gi, pl.ds(j * 128, 128), :])

    def pick(start_at, base, width):
        v = dmat[pl.ds(base, 16), pl.ds(0, width)]
        for t in range(1, 4):
            v = lax.select(start_at == 16 * t, dmat[pl.ds(base + 16 * t, 16), pl.ds(0, width)], v)
        return v

    def bases(q):
        for b in range(2):
            for a in range(4):
                hi, lo = split(pick(rows[a, 2 * q + b], 64 * a, 256))
                rst[q, 0, pl.ds(64 * b + 16 * a, 16)] = hi
                rst[q, 1, pl.ds(64 * b + 16 * a, 16)] = lo
                hi, lo = split(pick(cols[a, 2 * q + b], 64 * b, 128))
                for n, v in enumerate((hi, hi, lo)):
                    at = 32 * a + 16 * b
                    wk[q, pl.ds(at, 16), pl.ds(128 * n, 128)] = v
                    wr[q, pl.ds(128 * n + at, 16)] = v
        hi, lo = jnp.transpose(rst[q, 0]), jnp.transpose(rst[q, 1])
        for n, v in enumerate((hi, lo, hi)):
            rt[q, :, pl.ds(128 * n, 128)] = v
        far_h = ht[ng - 1, :, pl.ds(2 * td + pad, 2 * td)]
        hi, lo = split(mm(rst[q, 0], far_h) + mm(rst[q, 1], far_h))
        rh[q, pl.ds(0, 128)] = hi
        rh[q, pl.ds(128, 128)] = lo

    lane = lax.broadcasted_iota(jnp.int32, (64, 128), 1)
    lane16 = lax.broadcasted_iota(jnp.int32, (16, 128), 1)

    def of_row(a, v):
        return jnp.where(jnp.logical_and(lane16 >= 32 * a, lane16 < 32 * a + 32), v, 0.0)

    def near_part(q):
        g[q] += mm(ht[ng - 1, :, pl.ds(0, 2 * td)], o[q, ng - 1, pl.ds(0, 2 * td)])

    def far_part(q):
        far_h = ht[ng - 1, :, pl.ds(2 * td + pad, 2 * td)]
        return mm(far_h, o[q, ng - 1, pl.ds(2 * td + pad, 2 * td)])

    def partial(q):
        yp[q] = mm3(mm, (rst[q, 0], rst[q, 1]), split(g[q]))

    def analyse(q):
        v = mm(rh[q], o[q, ng - 1, pl.ds(2 * td + pad, 2 * td)])
        yst = yp[q] + (v[0:128] + v[128:256])
        hi, lo = split(jnp.where(lane < 64, yst[0:64], yst[64:128]))
        v = mmt(jnp.concatenate([hi, lo, hi], axis=1), wk[q])
        return sum(of_row(a, v[16 * a:16 * a + 16]) for a in range(1, 4)) + of_row(0, v[0:16])

    def lift(q, bands):
        hi, lo = split(jnp.concatenate([of_row(a, bands) for a in range(4)], axis=0))
        v = mm(jnp.concatenate([hi, lo, hi], axis=1), wr[q])
        v = jnp.concatenate([jnp.where(lane < 64, v, 0.0), jnp.where(lane < 64, 0.0, v)], axis=0)
        hi, lo = split(v)
        return mm(rt[q], jnp.concatenate([hi, hi, lo], axis=0))

    def axis(q, phase):
        return "y" if (q in Y_FIRST) == (phase == 0) else "x"

    def peer(name, i):
        return along_x(i) if name == "x" else along_y(i)

    size = {"x": nx, "y": ny}
    inbox = {"x": xbuf, "y": ybuf}
    place_of = {"x": x, "y": y}
    arrived = {"x": x_r, "y": y_r}
    sent = {"x": send_s.at[4], "y": send_s.at[5]}

    def spread(q, phase, src, value):
        name = axis(q, phase)
        n = size[name]
        for i in sorted(range(1, n), key=lambda i: -min(i, n - i)):
            remote(src.at[q], inbox[name].at[q, place_of[name]], sent[name], arrived[name].at[q], peer(name, i)).start()
        inbox[name][q, place_of[name]] = value

    def collect(q, phase):
        name = axis(q, phase)
        n, buf = size[name], inbox[name]
        if n > 1:
            drain(buf.at[q, pl.ds(0, n - 1)], arrived[name].at[q])
        s = buf[q, 0]
        for i in range(1, n):
            s = s + buf[q, i]
        return s

    def first_phase(q):
        v = analyse(q)
        band[q] = v
        spread(q, 0, band, v)

    def second_phase(q):
        s = collect(q, 0)
        xsum[q] = s
        spread(q, 1, xsum, s)

    def keep(q):
        mom_out[0, :, pl.ds(q * QW, QW)] = g[q] + far_part(q) - lift(q, band[q])

    def finish(q):
        upd_out[:, pl.ds(q * QW, QW)] = lift(q, collect(q, 1)).astype(bf16)

    def arrive(q, h):
        if h < ng - 1:
            for side in range(2):
                here = slot(q, h, side)
                ring(q, h, side, here).wait_recv()
                if h + 1 < ng - 1:
                    ring(q, h + 1, side, here).start()
                hand(q, h, side, here).start()
            if h + 1 == ng - 1:
                send_far(q, (slot(q, h, 0), slot(q, h, 1)))
        else:
            here = slot(q, h, 1)
            far(q, 0, here).wait_recv()
            hand(q, h, 1, here).start()

    def gather(q, h):
        if h < ng - 1:
            drain(o.at[q, h, pl.ds(2 * td, 2 * td)], part_r.at[q, h])
            g[q] += mm(ht[h, :, pl.ds(0, 4 * td)], o[q, h, pl.ds(0, 4 * td)])
            if h == ng - 2:
                partial(q)
        else:
            drain(slot(q, h, 3), part_r.at[q, h])

    for c in consts:
        c.wait()
    turn(ng - 1)
    drain(g, loc.at[4])
    drain(o.at[:, ng - 1, pl.ds(0, td)], loc.at[3])
    drain(o.at[:, ng - 1, pl.ds(0, td)], loc.at[5 + ng])
    for q in range(NQ):
        g[q] = 0.9 * g[q]
        near_part(q)
        if ng == 1:
            bases(q)
            partial(q)

    extra = [functools.partial(turn, gi) for gi in range(1, ng - 1)]
    if ng > 1:
        turn(0)
        extra += [functools.partial(bases, q) for q in range(NQ)]
    prior = None
    for h in range(ng):
        for q in range(NQ):
            arrive(q, h)
            if extra and (h or ng == 1):
                extra.pop(0)()
                if ng < 4:
                    while extra:
                        extra.pop(0)()
            if prior is not None:
                gather(*prior)
                if prior[1] == ng - 1:
                    first_phase(prior[0])
            prior = (q, h)
    gather(*prior)
    first_phase(NQ - 1)
    keep(0)
    for q in SECOND:
        second_phase(q)
    for q in range(1, NQ):
        keep(q)
    for q in LAST:
        finish(q)
    if ng > 1:
        drain(o.at[:, pl.ds(0, ng - 1), pl.ds(0, 2 * td)], send_s.at[0])
    for side, go in enumerate((go_right, go_left)):
        @pl.when(go)
        def _(side=side):
            drain(o.at[:, ng - 1, pl.ds(0, td)], send_s.at[1 + side])
    drain(o.at[:, :, pl.ds(0, 2 * td)], send_s.at[3])
    if nx > 1:
        drain(xbuf.at[:, pl.ds(0, nx - 1)], send_s.at[4])
    if ny > 1:
        drain(ybuf.at[:, pl.ds(0, ny - 1)], send_s.at[5])


def out_kernel(mom_in, upd_in, mom_out, upd_out, sems):
    def copies(k):
        part = pl.ds(k * (256 // PARTS), 256 // PARTS)
        return (
            pltpu.make_async_copy(mom_in.at[0, part], mom_out.at[0, part], sems.at[0, k]),
            pltpu.make_async_copy(upd_in.at[part], upd_out.at[part], sems.at[1, k]),
        )

    for k in range(PARTS):
        for c in copies(k):
            c.start()
    for k in range(PARTS):
        for c in copies(k):
            c.wait()


def build(dims, td):
    ny, nx, nz = dims
    ng = nz // 2
    dma = pltpu.SemaphoreType.DMA
    n_greet = max(1, (nx // 2 - 1 if nx > 1 else 0) + (ny // 2 - 1 if ny > 1 else 0))
    rows_all = 4 * td + 2 * (-2 * td % 128)
    anyspace = pl.BlockSpec(memory_space=pl.ANY)
    hbm = pl.BlockSpec(memory_space=pltpu.HBM)
    vmem = pl.BlockSpec(memory_space=pltpu.VMEM)
    step = pl.pallas_call(
        functools.partial(kernel, dims, td),
        name="demo_step",
        out_shape=(
            jax.ShapeDtypeStruct((1, 256, 512), f32),
            jax.ShapeDtypeStruct((256, 512), bf16),
        ),
        in_specs=[hbm] * 6,
        out_specs=(vmem, vmem),
        scratch_shapes=[
            pltpu.VMEM((ng, rows_all, 256), bf16),
            pltpu.VMEM((ng, 256, rows_all), bf16),
            pltpu.VMEM((NQ, ng, rows_all, QW), bf16),
            pltpu.VMEM((NQ, 256, QW), f32),
            pltpu.VMEM((NQ, 2, 128, 256), bf16),
            pltpu.VMEM((NQ, 256, 384), bf16),
            pltpu.VMEM((NQ, 128, 384), bf16),
            pltpu.VMEM((NQ, 384, 128), bf16),
            pltpu.VMEM((NQ, 256, 2 * td), bf16),
            pltpu.VMEM((NQ, 128, 128), f32),
            pltpu.VMEM((NQ, 16, 128), f32),
            pltpu.VMEM((NQ, nx, 16, 128), f32),
            pltpu.VMEM((NQ, 16, 128), f32),
            pltpu.VMEM((NQ, ny, 16, 128), f32),
            pltpu.VMEM((256, 256), f32),
            pltpu.SMEM((4, 8), jnp.int32),
            pltpu.SMEM((4, 8), jnp.int32),
            dma((6,)),
            dma((NQ, 2 * ng - 1)),
            dma((NQ, ng)),
            dma((NQ,)),
            dma((NQ,)),
            dma((6 + ng,)),
            pltpu.SemaphoreType.REGULAR((n_greet,)),
        ],
        compiler_params=pltpu.CompilerParams(
            collective_id=0, has_side_effects=True, vmem_limit_bytes=28 * 2**20
        ),
    )
    out = pl.pallas_call(
        out_kernel,
        name="results_out",
        out_shape=(
            jax.ShapeDtypeStruct((1, 256, 512), f32),
            jax.ShapeDtypeStruct((256, 512), bf16),
        ),
        in_specs=[anyspace, anyspace],
        out_specs=(anyspace, anyspace),
        scratch_shapes=[dma((2, PARTS))],
        compiler_params=pltpu.CompilerParams(vmem_limit_bytes=2**20),
    )
    return lambda *args: out(*step(*[pltpu.with_memory_space_constraint(a, pltpu.HBM) for a in args]))


def solution(mesh):
    n_rep, n_tp = mesh.shape["rep"], mesh.shape["tp"]
    dims = (n_rep // NX, NX, n_tp // 2)

    def local(hidden, out_grad, momentum, band_rows, band_start_columns):
        call = build(dims, out_grad.shape[0])
        return call(out_grad, hidden, momentum, band_rows, band_start_columns, jnp.asarray(block_basis()))

    return jax.shard_map(
        local,
        mesh=mesh,
        in_specs=(
            P("rep", "tp"),
            P(("rep", "tp"), None),
            P("rep", "tp", None),
            P("tp", None),
            P("tp", None),
        ),
        out_specs=(P("rep", "tp", None), P("tp", None)),
        check_vma=False,
    )
```

```python
import functools

import jax
import jax.numpy as jnp
import numpy as np
from jax import lax
from jax.experimental import pallas as pl
from jax.experimental.pallas import tpu as pltpu
from jax.sharding import PartitionSpec as P

MESH = pl.DeviceIdType.MESH
NX = 4
NQ = 4
QW = 128
PARTS = 4
Y_FIRST = (0, 2)
SECOND = (1, 0, 3, 2)
LAST = (0, 1, 2, 3)
f32 = jnp.float32
bf16 = jnp.bfloat16


def block_basis():
    k = np.arange(64)[:, None].astype(np.float64)
    n = np.arange(64)[None, :].astype(np.float64)
    scale = np.where(k == 0, np.sqrt(1.0 / 64), np.sqrt(2.0 / 64))
    b = scale * np.cos(np.pi * (n + 0.5) * k / 64)
    return np.kron(np.eye(4), b).astype(np.float32)


def split(v):
    hi = v.astype(bf16)
    return hi, (v - hi.astype(f32)).astype(bf16)


def mm(a, b):
    return lax.dot_general(a, b, (((1,), (0,)), ((), ())), preferred_element_type=f32)


def mmt(a, b):
    return lax.dot_general(a, b, (((1,), (1,)), ((), ())), preferred_element_type=f32)


def mm3(dot, a, b):
    (ah, al), (bh, bl) = a, b
    return dot(ah, bh) + (dot(ah, bl) + dot(al, bh))


def kernel(
    dims, td,
    og, hid, mom, rows_any, cols_any, dmat_any,
    mom_out, upd_out,
    hperm, ht, o, g, rst, rt, wk, wr, rh, yp, band, xbuf, xsum, ybuf, dmat, rows, cols,
    send_s, ring_r, part_r, x_r, y_r, loc, greet,
):
    ny, nx, nz = dims
    ng = nz // 2
    rep = lax.axis_index("rep")
    tp = lax.axis_index("tp")
    y, x = rep // nx, rep % nx
    z, core = tp // 2, tp % 2

    def from_right(chip):
        return jnp.logical_or(core == 1, lax.rem(chip + nz, nz) < nz // 8)

    go_right = jnp.logical_not(from_right(z + 1))
    go_left = from_right(z - 1)

    def along_z(k):
        return (rep, lax.rem(z + k + nz, nz) * 2 + core)

    def along_x(k):
        return (y * nx + lax.rem(x + k + nx, nx), tp)

    def along_y(k):
        return (lax.rem(y + k + ny, ny) * nx + x, tp)

    partner = (rep, z * 2 + 1 - core)

    def local(src, dst, n):
        return pltpu.make_async_copy(src, dst, loc.at[n])

    consts = [local(dmat_any, dmat, 0), local(rows_any, rows, 1), local(cols_any, cols, 2)]
    pad = -2 * td % 128

    def place(gi, k):
        if gi < ng - 1:
            return k * td
        return (0, 2 * td + pad, td, 3 * td + pad)[k]

    own_o = [local(og.at[:, pl.ds(q * QW, QW)], o.at[q, ng - 1, pl.ds(0, td)], 3) for q in range(NQ)]
    own_g = [local(mom.at[0, :, pl.ds(q * QW, QW)], g.at[q], 4) for q in range(NQ)]
    own_h = []
    for gi in range(ng):
        for k in range(4):
            if gi < ng - 1:
                chip = z - (gi + 1) if k % 2 == 0 else z + (gi + 1)
            else:
                chip = z if k % 2 == 0 else z + nz // 2
            c = core if k < 2 else 1 - core
            t = lax.rem(chip + nz, nz) * 2 + c
            own_h.append(
                local(hid.at[pl.ds(pl.multiple_of(t * td, 32), td)], hperm.at[gi, pl.ds(place(gi, k), td)], 5 + gi)
            )

    def drain(view, sem):
        pltpu.make_async_copy(view, view, sem).wait()

    near = [along_z(1), along_z(-1), partner]
    if nx > 1:
        near += [along_x(1), along_x(-1)]
    if ny > 1:
        near += [along_y(1), along_y(-1)]
    barrier = pltpu.get_barrier_semaphore()
    for d in near:
        pl.semaphore_signal(barrier, inc=1, device_id=d, device_id_type=MESH)
    pl.semaphore_wait(barrier, len(near))

    def remote(src, dst, ss, rs, dev):
        return pltpu.make_async_remote_copy(
            src_ref=src, dst_ref=dst, send_sem=ss, recv_sem=rs, device_id=dev, device_id_type=MESH
        )

    def slot(q, gi, k):
        return o.at[q, gi, pl.ds(place(gi, k), td)]

    def ring(q, h, side, src):
        return remote(src, slot(q, h, side), send_s.at[0], ring_r.at[q, 2 * h + side], along_z(1 - 2 * side))

    def far(q, side, src):
        return remote(src, slot(q, ng - 1, 1), send_s.at[1 + side], ring_r.at[q, 2 * ng - 2], along_z(1 - 2 * side))

    def hand(q, gi, k, src):
        own = gi == ng - 1 and k == 0
        return remote(src, slot(q, gi, k + 2), send_s.at[3], loc.at[5 + ng] if own else part_r.at[q, gi], partner)

    def send_far(q, sources):
        for side, go in enumerate((go_right, go_left)):
            @pl.when(go)
            def _(side=side):
                far(q, side, sources[side]).start()

    for q in range(NQ):
        src = og.at[:, pl.ds(q * QW, QW)]
        if ng > 1:
            ring(q, 0, 0, src).start()
            ring(q, 0, 1, src).start()
        else:
            send_far(q, (src, src))
        hand(q, ng - 1, 0, src).start()

    for c in consts + own_h[:4] + own_g + own_o + own_h[4:]:
        c.start()

    rounds = []
    if nx > 1:
        rounds += [(along_x, i) for i in range(nx // 2 - 1)]
    if ny > 1:
        rounds += [(along_y, i) for i in range(ny // 2 - 1)]
    for n, (axis, _) in enumerate(rounds):
        for k in (1, -1):
            pl.semaphore_signal(greet.at[n], inc=1, device_id=axis(k), device_id_type=MESH)
        pl.semaphore_wait(greet.at[n], 2)

    def turn(gi):
        drain(hperm.at[gi, pl.ds(0, 4 * td)], loc.at[5 + gi])
        for j in range((4 * td if gi < ng - 1 else 4 * td + 2 * pad) // 128):
            ht[gi, :, pl.ds(j * 128, 128)] = jnp.transpose(hperm[gi, pl.ds(j * 128, 128), :])

    def pick(start_at, base, width):
        v = dmat[pl.ds(base, 16), pl.ds(0, width)]
        for t in range(1, 4):
            v = lax.select(start_at == 16 * t, dmat[pl.ds(base + 16 * t, 16), pl.ds(0, width)], v)
        return v

    def bases(q):
        for b in range(2):
            for a in range(4):
                hi, lo = split(pick(rows[a, 2 * q + b], 64 * a, 256))
                rst[q, 0, pl.ds(64 * b + 16 * a, 16)] = hi
                rst[q, 1, pl.ds(64 * b + 16 * a, 16)] = lo
                hi, lo = split(pick(cols[a, 2 * q + b], 64 * b, 128))
                for n, v in enumerate((hi, hi, lo)):
                    at = 32 * a + 16 * b
                    wk[q, pl.ds(at, 16), pl.ds(128 * n, 128)] = v
                    wr[q, pl.ds(128 * n + at, 16)] = v
        hi, lo = jnp.transpose(rst[q, 0]), jnp.transpose(rst[q, 1])
        for n, v in enumerate((hi, lo, hi)):
            rt[q, :, pl.ds(128 * n, 128)] = v
        far_h = ht[ng - 1, :, pl.ds(2 * td + pad, 2 * td)]
        hi, lo = split(mm(rst[q, 0], far_h) + mm(rst[q, 1], far_h))
        rh[q, pl.ds(0, 128)] = hi
        rh[q, pl.ds(128, 128)] = lo

    lane = lax.broadcasted_iota(jnp.int32, (64, 128), 1)
    lane16 = lax.broadcasted_iota(jnp.int32, (16, 128), 1)

    def of_row(a, v):
        return jnp.where(jnp.logical_and(lane16 >= 32 * a, lane16 < 32 * a + 32), v, 0.0)

    def near_part(q):
        g[q] += mm(ht[ng - 1, :, pl.ds(0, 2 * td)], o[q, ng - 1, pl.ds(0, 2 * td)])

    def far_part(q):
        far_h = ht[ng - 1, :, pl.ds(2 * td + pad, 2 * td)]
        return mm(far_h, o[q, ng - 1, pl.ds(2 * td + pad, 2 * td)])

    def partial(q):
        yp[q] = mm3(mm, (rst[q, 0], rst[q, 1]), split(g[q]))

    def analyse(q):
        v = mm(rh[q], o[q, ng - 1, pl.ds(2 * td + pad, 2 * td)])
        yst = yp[q] + (v[0:128] + v[128:256])
        hi, lo = split(jnp.where(lane < 64, yst[0:64], yst[64:128]))
        v = mmt(jnp.concatenate([hi, lo, hi], axis=1), wk[q])
        return sum(of_row(a, v[16 * a:16 * a + 16]) for a in range(1, 4)) + of_row(0, v[0:16])

    def lift(q, bands):
        hi, lo = split(jnp.concatenate([of_row(a, bands) for a in range(4)], axis=0))
        v = mm(jnp.concatenate([hi, lo, hi], axis=1), wr[q])
        v = jnp.concatenate([jnp.where(lane < 64, v, 0.0), jnp.where(lane < 64, 0.0, v)], axis=0)
        hi, lo = split(v)
        return mm(rt[q], jnp.concatenate([hi, hi, lo], axis=0))

    def axis(q, phase):
        return "y" if (q in Y_FIRST) == (phase == 0) else "x"

    def peer(name, i):
        return along_x(i) if name == "x" else along_y(i)

    size = {"x": nx, "y": ny}
    inbox = {"x": xbuf, "y": ybuf}
    place_of = {"x": x, "y": y}
    arrived = {"x": x_r, "y": y_r}
    sent = {"x": send_s.at[4], "y": send_s.at[5]}

    def spread(q, phase, src, value):
        name = axis(q, phase)
        n = size[name]
        for i in sorted(range(1, n), key=lambda i: -min(i, n - i)):
            remote(src.at[q], inbox[name].at[q, place_of[name]], sent[name], arrived[name].at[q], peer(name, i)).start()
        inbox[name][q, place_of[name]] = value

    def collect(q, phase):
        name = axis(q, phase)
        n, buf = size[name], inbox[name]
        if n > 1:
            drain(buf.at[q, pl.ds(0, n - 1)], arrived[name].at[q])
        s = buf[q, 0]
        for i in range(1, n):
            s = s + buf[q, i]
        return s

    def first_phase(q):
        v = analyse(q)
        band[q] = v
        spread(q, 0, band, v)

    def second_phase(q):
        s = collect(q, 0)
        xsum[q] = s
        spread(q, 1, xsum, s)

    def keep(q):
        mom_out[0, :, pl.ds(q * QW, QW)] = g[q] + far_part(q) - lift(q, band[q])

    def finish(q):
        upd_out[:, pl.ds(q * QW, QW)] = lift(q, collect(q, 1)).astype(bf16)

    def arrive(q, h):
        if h < ng - 1:
            for side in range(2):
                here = slot(q, h, side)
                ring(q, h, side, here).wait_recv()
                if h + 1 < ng - 1:
                    ring(q, h + 1, side, here).start()
                hand(q, h, side, here).start()
            if h + 1 == ng - 1:
                send_far(q, (slot(q, h, 0), slot(q, h, 1)))
        else:
            here = slot(q, h, 1)
            far(q, 0, here).wait_recv()
            hand(q, h, 1, here).start()

    def gather(q, h):
        if h < ng - 1:
            drain(o.at[q, h, pl.ds(2 * td, 2 * td)], part_r.at[q, h])
            g[q] += mm(ht[h, :, pl.ds(0, 4 * td)], o[q, h, pl.ds(0, 4 * td)])
            if h == ng - 2:
                partial(q)
        else:
            drain(slot(q, h, 3), part_r.at[q, h])

    for c in consts:
        c.wait()
    turn(ng - 1)
    drain(g, loc.at[4])
    drain(o.at[:, ng - 1, pl.ds(0, td)], loc.at[3])
    drain(o.at[:, ng - 1, pl.ds(0, td)], loc.at[5 + ng])
    for q in range(NQ):
        g[q] = 0.9 * g[q]
        near_part(q)
        if ng == 1:
            bases(q)
            partial(q)

    extra = [functools.partial(turn, gi) for gi in range(1, ng - 1)]
    if ng > 1:
        turn(0)
        extra += [functools.partial(bases, q) for q in range(NQ)]
    prior = None
    for h in range(ng):
        for q in range(NQ):
            arrive(q, h)
            if extra and (h or ng == 1):
                extra.pop(0)()
                if ng < 4:
                    while extra:
                        extra.pop(0)()
            if prior is not None:
                gather(*prior)
                if prior[1] == ng - 1:
                    first_phase(prior[0])
            prior = (q, h)
    gather(*prior)
    first_phase(NQ - 1)
    keep(0)
    for q in SECOND:
        second_phase(q)
    for q in range(1, NQ):
        keep(q)
    for q in LAST:
        finish(q)
    if ng > 1:
        drain(o.at[:, pl.ds(0, ng - 1), pl.ds(0, 2 * td)], send_s.at[0])
    for side, go in enumerate((go_right, go_left)):
        @pl.when(go)
        def _(side=side):
            drain(o.at[:, ng - 1, pl.ds(0, td)], send_s.at[1 + side])
    drain(o.at[:, :, pl.ds(0, 2 * td)], send_s.at[3])
    if nx > 1:
        drain(xbuf.at[:, pl.ds(0, nx - 1)], send_s.at[4])
    if ny > 1:
        drain(ybuf.at[:, pl.ds(0, ny - 1)], send_s.at[5])


def out_kernel(mom_in, upd_in, mom_out, upd_out, sems):
    def copies(k):
        part = pl.ds(k * (256 // PARTS), 256 // PARTS)
        return (
            pltpu.make_async_copy(mom_in.at[0, part], mom_out.at[0, part], sems.at[0, k]),
            pltpu.make_async_copy(upd_in.at[part], upd_out.at[part], sems.at[1, k]),
        )

    for k in range(PARTS):
        for c in copies(k):
            c.start()
    for k in range(PARTS):
        for c in copies(k):
            c.wait()


def build(dims, td):
    ny, nx, nz = dims
    ng = nz // 2
    dma = pltpu.SemaphoreType.DMA
    n_greet = max(1, (nx // 2 - 1 if nx > 1 else 0) + (ny // 2 - 1 if ny > 1 else 0))
    rows_all = 4 * td + 2 * (-2 * td % 128)
    anyspace = pl.BlockSpec(memory_space=pl.ANY)
    hbm = pl.BlockSpec(memory_space=pltpu.HBM)
    vmem = pl.BlockSpec(memory_space=pltpu.VMEM)
    step = pl.pallas_call(
        functools.partial(kernel, dims, td),
        name="demo_step",
        out_shape=(
            jax.ShapeDtypeStruct((1, 256, 512), f32),
            jax.ShapeDtypeStruct((256, 512), bf16),
        ),
        in_specs=[hbm] * 6,
        out_specs=(vmem, vmem),
        scratch_shapes=[
            pltpu.VMEM((ng, rows_all, 256), bf16),
            pltpu.VMEM((ng, 256, rows_all), bf16),
            pltpu.VMEM((NQ, ng, rows_all, QW), bf16),
            pltpu.VMEM((NQ, 256, QW), f32),
            pltpu.VMEM((NQ, 2, 128, 256), bf16),
            pltpu.VMEM((NQ, 256, 384), bf16),
            pltpu.VMEM((NQ, 128, 384), bf16),
            pltpu.VMEM((NQ, 384, 128), bf16),
            pltpu.VMEM((NQ, 256, 2 * td), bf16),
            pltpu.VMEM((NQ, 128, 128), f32),
            pltpu.VMEM((NQ, 16, 128), f32),
            pltpu.VMEM((NQ, nx, 16, 128), f32),
            pltpu.VMEM((NQ, 16, 128), f32),
            pltpu.VMEM((NQ, ny, 16, 128), f32),
            pltpu.VMEM((256, 256), f32),
            pltpu.SMEM((4, 8), jnp.int32),
            pltpu.SMEM((4, 8), jnp.int32),
            dma((6,)),
            dma((NQ, 2 * ng - 1)),
            dma((NQ, ng)),
            dma((NQ,)),
            dma((NQ,)),
            dma((6 + ng,)),
            pltpu.SemaphoreType.REGULAR((n_greet,)),
        ],
        compiler_params=pltpu.CompilerParams(
            collective_id=0, has_side_effects=True, vmem_limit_bytes=28 * 2**20
        ),
    )
    out = pl.pallas_call(
        out_kernel,
        name="results_out",
        out_shape=(
            jax.ShapeDtypeStruct((1, 256, 512), f32),
            jax.ShapeDtypeStruct((256, 512), bf16),
        ),
        in_specs=[anyspace, anyspace],
        out_specs=(anyspace, anyspace),
        scratch_shapes=[dma((2, PARTS))],
        compiler_params=pltpu.CompilerParams(vmem_limit_bytes=2**20),
    )
    return lambda *args: out(*step(*[pltpu.with_memory_space_constraint(a, pltpu.HBM) for a in args]))


def solution(mesh):
    n_rep, n_tp = mesh.shape["rep"], mesh.shape["tp"]
    dims = (n_rep // NX, NX, n_tp // 2)

    def local(hidden, out_grad, momentum, band_rows, band_start_columns):
        call = build(dims, out_grad.shape[0])
        return call(out_grad, hidden, momentum, band_rows, band_start_columns, jnp.asarray(block_basis()))

    return jax.shard_map(
        local,
        mesh=mesh,
        in_specs=(
            P("rep", "tp"),
            P(("rep", "tp"), None),
            P("rep", "tp", None),
            P("tp", None),
            P("tp", None),
        ),
        out_specs=(P("rep", "tp", None), P("tp", None)),
        check_vma=False,
    )
```
